32 devices in a mesh: groups: 2 (over y), tile: 4 (over z), det: 2 (over x), band: 2 (over core).
Axes of the slice: x: 2, y: 2, z: 4, core: 2. Of those that a mesh axis runs over, the one named last changes fastest.
Arguments:
- left_raw: float32 [128, 512], P(('groups', 'tile'), 'det'), parts along dimension 0
- right_raw: float32 [128, 512], P(('groups', 'tile'), 'det'), parts along dimension 0
- line_offset: int32 [1024], P(('groups', 'det')), parts along dimension 0, may hold values from -8 to 8, as said below
- pair_count: int32 [8], P(('groups', 'tile')), parts along dimension 0, may hold values from 1 to 2, as said below
- pair_tile: int32 [8, 2], P(('groups', 'tile')), parts along dimension 0, may hold values from 0 to 3, as said below
- pair_base: int32 [8, 2], P(('groups', 'tile')), parts along dimension 0, may hold values from 0 to 32, as said below
Outputs:
- disparity: float32 [8, 2, 16, 512], P(('groups', 'tile'), None, 'det'), parts along dimension 0
The draws below stay inside these ranges and needn't reach their ends.
There are 2 independent parts, one for each index of `groups`. The reference program is written for one: setup_inputs(seed, part) draws one part's arguments, and reference() takes and returns one part's arrays. A program takes and returns all parts, laid end to end along the dimension named above; each array names one. Nothing has to cross between parts.
Inputs may be any that keep to these rules, and one draw needn't show every extreme that they name: `line_offset`: some column has offset 8 and some column -8. `pair_count`: number of live slots of a tile; slots from this number on are empty. Some tile has 2 live slots and some tile one. `pair_tile`: every entry lies within 2 tiles of its own tile; a live slot reaches 2 tiles back, and some slot reaches 2 tiles ahead. `pair_base`: some pair has offset 32.
All inputs are finite; a program needn't handle non-finite values.
Results may differ from the reference program's by a relative error of at most 0.0003.
Values sent between devices are 32-bit elements; how exact they have to be, the bound alone decides.
No kernel may reach another device: no remote copies, remote signals or barrier semaphores. Data moves between devices by JAX's collectives and lax.ppermute only.
A program may use at most 64 MiB of HBM per device.

```python
import jax
import jax.numpy as jnp
from jax import lax

W = 512
DISP = 128
WIN = 15
PMAX = 2
REACH = 2
OMAX = 8
BMAX = 32
LT = 16
NTILES = 4
NL = 64


def image_draw(seed_key):
    subkeys = jax.random.split(seed_key, 3)
    row_scale = jnp.exp(jax.random.uniform(subkeys[1], (NL, 1), jnp.float32, -1.2, 1.2))
    col_scale = jnp.exp(jax.random.uniform(subkeys[2], (1, W), jnp.float32, -1.2, 1.2))
    noise_field = jax.random.normal(subkeys[0], (NL, W), jnp.float32)
    return noise_field * row_scale * col_scale


def draw_left_raw(key, part):
    return image_draw(jax.random.fold_in(key, 11))


def draw_right_raw(key, part):
    return image_draw(jax.random.fold_in(key, 23))


def draw_line_offset(key, part):
    subkeys = jax.random.split(jax.random.fold_in(key, 31), 2)
    base_offsets = jax.random.randint(subkeys[0], (W,), -OMAX, OMAX + 1, jnp.int32)
    shuffled = jax.random.permutation(subkeys[1], W)
    base_offsets = base_offsets.at[shuffled[0]].set(OMAX)
    return base_offsets.at[shuffled[1]].set(-OMAX)


def draw_pair_count(key, part):
    subkeys = jax.random.split(jax.random.fold_in(key, 41), 2)
    counts_drawn = jax.random.randint(subkeys[0], (NTILES,), 1, PMAX + 1, jnp.int32)
    shuffled = jax.random.permutation(subkeys[1], NTILES)
    counts_drawn = counts_drawn.at[shuffled[0]].set(PMAX)
    return counts_drawn.at[shuffled[1]].set(1)


def draw_pair_tile(key, part):
    subkeys = jax.random.split(jax.random.fold_in(key, 53), 3)
    tile_ids = jnp.arange(NTILES, dtype=jnp.int32)[:, None]
    tile_steps = jax.random.randint(subkeys[0], (NTILES, PMAX), -REACH, REACH + 1, jnp.int32)
    partner = jnp.clip(tile_ids + tile_steps, 0, NTILES - 1).astype(jnp.int32)
    lower_tile = jax.random.randint(subkeys[1], (), REACH, NTILES, jnp.int32)
    upper_tile = jax.random.randint(subkeys[2], (), 0, NTILES - REACH, jnp.int32)
    partner = partner.at[lower_tile, 0].set(lower_tile - REACH)
    return partner.at[upper_tile, PMAX - 1].set(upper_tile + REACH)


def draw_pair_base(key, part):
    subkeys = jax.random.split(jax.random.fold_in(key, 67), 2)
    offsets_drawn = jax.random.randint(subkeys[0], (NTILES, PMAX), 0, BMAX + 1, jnp.int32)
    chosen_tile = jax.random.randint(subkeys[1], (), 0, NTILES, jnp.int32)
    return offsets_drawn.at[chosen_tile, 0].set(BMAX)


def setup_inputs(seed: int = 0, part: int = 0) -> dict:
    keys = jax.random.split(jax.random.key(seed), 7)
    part_splits = jax.random.split(jax.random.fold_in(keys[6], part), 7)
    left_raw = draw_left_raw(jax.random.fold_in(jax.random.fold_in(keys[6], part), 71), part)
    right_raw = draw_right_raw(jax.random.fold_in(jax.random.fold_in(keys[6], part), 71), part)
    line_offset = draw_line_offset(jax.random.fold_in(jax.random.fold_in(keys[6], part), 71), part)
    pair_count = draw_pair_count(jax.random.fold_in(jax.random.fold_in(keys[6], part), 71), part)
    pair_tile = draw_pair_tile(jax.random.fold_in(jax.random.fold_in(keys[6], part), 71), part)
    pair_base = draw_pair_base(jax.random.fold_in(jax.random.fold_in(keys[6], part), 71), part)
    return dict(left_raw=left_raw, right_raw=right_raw, line_offset=line_offset, pair_count=pair_count, pair_tile=pair_tile, pair_base=pair_base)


REG = 0.1
SHARP = 30.0

def band_ones(size_in, size_out):
    source_ids = jnp.arange(size_in, dtype=jnp.int32)[:, None]
    target_ids = jnp.arange(size_out, dtype=jnp.int32)[None, :]
    offset_ids = source_ids - target_ids
    return ((offset_ids >= 0) & (offset_ids < WIN)).astype(jnp.float32)

def box_sum(volume):
    rows_in = volume.shape[-2]
    cols_in = volume.shape[-1]
    across = jnp.matmul(volume, band_ones(cols_in, cols_in - WIN + 1), precision=lax.Precision.HIGHEST)
    downward = band_ones(rows_in, rows_in - WIN + 1).T
    return jnp.matmul(downward, across, precision=lax.Precision.HIGHEST)

def pair_sums(left_ext, right_ext, base_cols, band_first, band_width, block_width):
    margin = (WIN - 1) // 2
    tile_cols = left_ext.shape[1]
    left_pad = jnp.pad(left_ext, ((0, 0), (margin, margin)))
    lead_cols = BMAX + DISP + margin
    right_pad = jnp.pad(right_ext, ((0, 0), (lead_cols, margin)))
    start_col = (lead_cols - margin - band_width + 1 - band_first - base_cols).astype(jnp.int32)
    window = lax.dynamic_slice_in_dim(right_pad, start_col, tile_cols + 2 * margin + band_width - 1, 1)
    window_cells = float(WIN * WIN)
    left_mean = box_sum(left_pad) / window_cells
    left_var = box_sum(left_pad * left_pad) / window_cells - left_mean * left_mean
    wide_sums = box_sum(jnp.stack([window, window * window]))

    def block_step(block_id, totals):
        weight_sum, moment_sum = totals
        disparity_ids = block_id * block_width + jnp.arange(block_width, dtype=jnp.int32)
        shift_ids = (band_width - 1 - disparity_ids).astype(jnp.int32)

        def take_volume(shift_col):
            return lax.dynamic_slice_in_dim(window, shift_col, tile_cols + 2 * margin, 1)

        def take_stats(shift_col):
            return lax.dynamic_slice_in_dim(wide_sums, shift_col, tile_cols, 2)
        volume = jax.vmap(take_volume)(shift_ids)
        cross_sum = box_sum(left_pad[None] * volume)
        right_stats = jax.vmap(take_stats)(shift_ids)
        right_mean = right_stats[:, 0] / window_cells
        right_var = right_stats[:, 1] / window_cells - right_mean * right_mean
        covariance = cross_sum / window_cells - left_mean[None] * right_mean
        ncc_score = covariance / jnp.sqrt((left_var[None] + REG) * (right_var + REG))
        weight = jnp.exp(SHARP * ncc_score)
        disparity_values = (band_first + disparity_ids).astype(jnp.float32)[:, None, None]
        return (weight_sum + lax.optimization_barrier(jnp.sum(weight, axis=0)), moment_sum + lax.optimization_barrier(jnp.sum(weight * disparity_values, axis=0)))
    zeroed = jnp.zeros(left_mean.shape, jnp.float32)
    return lax.fori_loop(0, band_width // block_width, block_step, (zeroed, zeroed))

def reference(left_raw, right_raw, line_offset, pair_count, pair_tile, pair_base):
    margin = (WIN - 1) // 2
    target_lines = jnp.arange(NL, dtype=jnp.int32)[:, None] + line_offset[None, :].astype(jnp.int32)
    inside = (target_lines >= 0) & (target_lines < NL)
    clipped = jnp.clip(target_lines, 0, NL - 1).astype(jnp.int32)

    def resample(raw_image):
        picked = jnp.take_along_axis(raw_image, clipped, axis=0)
        return jnp.where(inside, picked, jnp.zeros_like(picked)).reshape(NTILES, LT, W)
    left_tiles = resample(left_raw)
    right_tiles = resample(right_raw)

    def single_pair(pair_index):
        tile_id = pair_index // PMAX
        slot_id = pair_index % PMAX
        partner = pair_tile[tile_id, slot_id]
        base_cols = pair_base[tile_id, slot_id]
        left_ext = jnp.pad(left_tiles[tile_id], ((margin, margin), (0, 0)))
        right_ext = jnp.pad(right_tiles[partner], ((margin, margin), (0, 0)))
        weight_sum, moment_sum = pair_sums(left_ext, right_ext, base_cols, 0, DISP, 16)
        disparity = (base_cols.astype(jnp.float32) + moment_sum / weight_sum) / DISP
        return jnp.where(slot_id < pair_count[tile_id], disparity, jnp.zeros_like(disparity))
    results = lax.map(single_pair, jnp.arange(NTILES * PMAX, dtype=jnp.int32))
    return results.reshape(NTILES, PMAX, LT, W)
```

```python
import functools

import jax
import jax.numpy as jnp
from jax import lax
from jax.experimental import pallas as pl
from jax.experimental.pallas import tpu as pltpu
from jax.sharding import PartitionSpec as P

DISP = 128
WIN = 15
PMAX = 2
REACH = 2
OMAX = 8

REG = 0.1
SHARP = 30.0

LANES = 128
SUB = 8
BLKS = 4
STEPS = DISP // SUB
VIEWS = BLKS + STEPS - 1


def lane_gather(source, index):
    return jnp.take_along_axis(source, index, axis=1)


def row_gather(source, index):
    return jnp.take_along_axis(source, index, axis=0)


def stereo_kernel(plan, *refs):
    n_in = plan["n_in"]
    ins = refs[:n_in]
    count_ref, partner_ref, base_ref = refs[n_in : n_in + 3]
    out_ref = refs[n_in + 3]
    strip, tiles, left_rows, left_stats, raw_stats, right_rows, right_stats, sums, outs, sem = refs[
        n_in + 4 :
    ]
    lines = plan["lines"]
    two_sided = plan["two_sided"]
    pad = plan["pad"]
    blocks = plan["blocks"]
    det = lax.axis_index("det")
    tile = lax.axis_index("tile")
    n_win = WIN - 1 + SUB if two_sided else SUB + WIN // 2

    copies = []
    for source, target in plan["copies"](ins, strip, tile, det):
        copy = pltpu.make_async_copy(source, target, sem.at[len(copies)])
        copy.start()
        copies.append(copy)

    lane = lax.broadcasted_iota(jnp.int32, (SUB, LANES), 1)
    row = lax.broadcasted_iota(jnp.int32, (SUB, LANES), 0)
    zero = jnp.zeros((SUB, LANES), jnp.float32)
    chunks = out_ref.shape[-1] // LANES
    per = LANES // BLKS
    for plane in range(2):
        for chunk in range(chunks):
            cols = slice(chunk * LANES, (chunk + 1) * LANES)
            strip[plane, 0:OMAX, cols] = zero
            strip[plane, OMAX + blocks * lines : 2 * OMAX + blocks * lines, cols] = zero
    if pad:
        for plane in range(2):
            for blk in range(BLKS):
                tiles[plane, blk, 0:SUB, :] = zero
                tiles[plane, blk, SUB + lines : 2 * SUB + lines, :] = zero
    offsets = plan["offsets"](ins, det)
    for copy in copies:
        copy.wait()

    def resample(plane, block):
        for group in range(lines // SUB):
            start = block * lines + group * SUB
            natural = []
            for chunk in range(chunks):
                cols = slice(chunk * LANES, (chunk + 1) * LANES)
                want = row + offsets[chunk] + OMAX
                index = want & (SUB - 1)
                part = want >> 3
                picked = [
                    row_gather(
                        strip[plane, pl.ds(pl.multiple_of(start + SUB * k, SUB), SUB), cols], index
                    )
                    for k in range(3)
                ]
                natural.append(
                    jnp.where(part == 0, picked[0], jnp.where(part == 1, picked[1], picked[2]))
                )
            for blk in range(BLKS):
                index = (BLKS * lane + blk) & (LANES - 1)
                value = lane_gather(natural[0], index)
                for chunk in range(1, chunks):
                    value = jnp.where(
                        lane >= chunk * per, lane_gather(natural[chunk], index), value
                    )
                tiles[plane, blk, pad + group * SUB : pad + group * SUB + SUB, :] = value

    def row_at(win):
        if not two_sided:
            return win + det * (lines - 1 - 2 * win)
        if win < SUB + WIN // 2:
            return pad + SUB * det + win
        return pad + SUB * det - 1 - (win - SUB - WIN // 2)

    def load_row(plane, blk, win):
        return jnp.broadcast_to(tiles[plane, blk, pl.ds(row_at(win), 1), :], (SUB, LANES))

    def up(value, count):
        return jnp.where(lane >= count, pltpu.roll(value, count, 1), 0.0)

    def down(value, count):
        return jnp.where(lane < LANES - count, pltpu.roll(value, LANES - count, 1), 0.0)

    def down_wrapped(value, count):
        return jnp.where(lane >= LANES - count, pltpu.roll(value, LANES - count, 1), 0.0)

    def partials(values):
        first2 = values[0] + values[1]
        first3 = first2 + values[2]
        last2 = values[2] + values[3]
        return first2, first3, first3 + values[3], last2, values[1] + last2

    def across(values):
        first2, first3, full, last2, last3 = partials(values)
        mid = full + up(full, 1) + down(full, 1)
        return [
            mid + up(last3, 2),
            (mid + up(last2, 2)) + down(values[0], 2),
            (mid + up(values[3], 2)) + down(first2, 2),
            mid + down(first3, 2),
        ]

    def across_before(values):
        first2, first3, full, _, _ = partials(values)
        mid = down_wrapped(full, 1)
        return [
            mid,
            mid + down_wrapped(values[0], 2),
            mid + down_wrapped(first2, 2),
            mid + down_wrapped(first3, 2),
        ]

    def each_line(product):
        current = []
        for blk in range(BLKS):
            total = product(0, blk)
            for win in range(1, SUB):
                total = total + product(win, blk)
            current.append(total)
        before = None
        if two_sided:
            before = [[zero] * BLKS]
            for j in range(WIN // 2):
                before.append(
                    [
                        before[-1][blk] + product(SUB + WIN // 2 + j, blk)
                        for blk in range(BLKS)
                    ]
                )
        for line in range(SUB):
            if line:
                current = [current[blk] + product(SUB + line - 1, blk) for blk in range(BLKS)]
            if two_sided:
                yield line, [current[blk] + before[SUB - 1 - line][blk] for blk in range(BLKS)]
            else:
                yield line, current

    cell = 1.0 / (WIN * WIN)

    def stats(total, squares):
        mean = total * cell
        return mean, lax.rsqrt((squares * cell - mean * mean) + REG)

    resample(0, plan["block_of"](tile, tile))
    for win in range(n_win):
        for blk in range(BLKS):
            left_rows[win, blk] = load_row(0, blk, win)
    plain = each_line(lambda win, blk: left_rows[win, blk])
    square = each_line(lambda win, blk: left_rows[win, blk] * left_rows[win, blk])
    for (line, total), (_, squares) in zip(plain, square):
        total = across(total)
        squares = across(squares)
        for blk in range(BLKS):
            mean, gain = stats(total[blk], squares[blk])
            left_stats[0, line, blk] = mean
            left_stats[1, line, blk] = gain * SHARP
    for win in range(n_win):
        for blk in range(BLKS):
            left_rows[win, blk] = left_rows[win, blk] * cell

    for slot in range(PMAX):
        for chunk in range(chunks):
            out_ref[0, slot, :, chunk * LANES : (chunk + 1) * LANES] = zero

    def run_slot(slot, carry):
        base = base_ref[0, slot]
        resample(1, plan["block_of"](partner_ref[0, slot], tile))
        right = [[load_row(1, blk, win) for blk in range(BLKS)] for win in range(n_win)]
        plain = each_line(lambda win, blk: right[win][blk])
        square = each_line(lambda win, blk: right[win][blk] * right[win][blk])
        for (line, total), (_, squares) in zip(plain, square):
            for part, function in enumerate((across, across_before)):
                part_total = function(total)
                part_squares = function(squares)
                for blk in range(BLKS):
                    mean, gain = stats(part_total[blk], part_squares[blk])
                    raw_stats[part, 0, line, blk] = mean
                    raw_stats[part, 1, line, blk] = gain

        def make_view(view, carry):
            shift = view - (STEPS - 1) - base
            blk = shift & (BLKS - 1)
            moved = (blk - shift) >> 2
            turn = moved + (STEPS // BLKS) * row
            wraps = lane >= LANES - turn
            source = (lane - turn) & (LANES - 1)

            def turned(value):
                return lane_gather(value, source)

            for win in range(n_win):
                value = jnp.broadcast_to(
                    tiles[1, blk, pl.ds(row_at(win), 1), :], (SUB, LANES)
                )
                right_rows[view, win] = turned(jnp.where(wraps, 0.0, value))
            for kind in range(2):
                for line in range(SUB):
                    right_stats[view, kind, line] = turned(
                        jnp.where(
                            wraps, raw_stats[1, kind, line, blk], raw_stats[0, kind, line, blk]
                        )
                    )
            return carry

        lax.fori_loop(0, VIEWS, make_view, 0)
        for line in range(SUB):
            for blk in range(BLKS):
                sums[0, line, blk] = zero
                sums[1, line, blk] = zero

        def step_body(count, carry):
            view = count
            for line, value in each_line(
                lambda win, blk: left_rows[win, blk] * right_rows[view + blk, win]
            ):
                for blk, total in enumerate(across(value)):
                    cov = total - left_stats[0, line, blk] * right_stats[view + blk, 0, line]
                    weight = jnp.exp(
                        (cov * left_stats[1, line, blk]) * right_stats[view + blk, 1, line]
                    )
                    held = sums[0, line, blk]
                    sums[1, line, blk] = sums[1, line, blk] + held
                    sums[0, line, blk] = held + weight
            return carry

        lax.fori_loop(0, STEPS, step_body, 0)
        scale = (row * STEPS).astype(jnp.float32)
        for line in range(SUB):
            for blk in range(BLKS):
                weights = sums[0, line, blk]
                moments = sums[1, line, blk] + scale * weights
                weight_sum = jnp.sum(weights, axis=0, keepdims=True)
                moment_sum = jnp.sum(moments, axis=0, keepdims=True)
                value = (base.astype(jnp.float32) + moment_sum / weight_sum) / DISP
                target = line if two_sided else line + det * (SUB - 1 - 2 * line)
                outs[blk, pl.ds(target, 1), :] = value
        for chunk in range(chunks):
            index = chunk * per + (lane >> 2)
            value = lane_gather(outs[0], index)
            for blk in range(1, BLKS):
                value = jnp.where(
                    (lane & (BLKS - 1)) == blk, lane_gather(outs[blk], index), value
                )
            out_ref[0, slot, :, chunk * LANES : (chunk + 1) * LANES] = value
        return carry

    lax.fori_loop(0, jnp.minimum(count_ref[0], PMAX), run_slot, 0)


def run_kernel(plan, ins, pair_count, pair_tile, pair_base, cols, specs):
    lines = plan["lines"]
    blocks = plan["blocks"]
    n_win = WIN - 1 + SUB if plan["two_sided"] else SUB + WIN // 2
    plan = dict(plan, n_in=len(ins))
    smem = pl.BlockSpec(memory_space=pltpu.SMEM)
    f32 = jnp.float32
    return pl.pallas_call(
        functools.partial(stereo_kernel, plan),
        out_shape=jax.ShapeDtypeStruct((1, PMAX, SUB, cols), f32),
        in_specs=list(specs) + [smem, smem, smem],
        out_specs=pl.BlockSpec(memory_space=pltpu.VMEM),
        scratch_shapes=[
            pltpu.VMEM((2, blocks * lines + 2 * OMAX, cols), f32),
            pltpu.VMEM((2, BLKS, lines + 2 * plan["pad"], LANES), f32),
            pltpu.VMEM((n_win, BLKS, SUB, LANES), f32),
            pltpu.VMEM((2, SUB, BLKS, SUB, LANES), f32),
            pltpu.VMEM((2, 2, SUB, BLKS, SUB, LANES), f32),
            pltpu.VMEM((VIEWS, n_win, SUB, LANES), f32),
            pltpu.VMEM((VIEWS, 2, SUB, SUB, LANES), f32),
            pltpu.VMEM((2, SUB, BLKS, SUB, LANES), f32),
            pltpu.VMEM((BLKS, SUB, LANES), f32),
            pltpu.SemaphoreType.DMA((plan["n_copies"],)),
        ],
        compiler_params=pltpu.CompilerParams(vmem_limit_bytes=32 << 20),
        name="stereo",
    )(*ins, pair_count, pair_tile, pair_base)


ANY = pl.BlockSpec(memory_space=pl.ANY)
VMEM = pl.BlockSpec(memory_space=pltpu.VMEM)


def xor_front(left_raw, right_raw, line_offset):
    tiles, dets, bands = (lax.axis_size(a) for a in ("tile", "det", "band"))
    lines, width = left_raw.shape

    def fetch(value, flip):
        pairs = []
        for t in range(tiles):
            for d in range(dets):
                for b in range(bands):
                    source = (t * dets + d) * bands + b
                    target = ((t ^ flip) * dets + (d ^ b)) * bands + b
                    pairs.append((source, target))
        return lax.ppermute(value, ("tile", "det", "band"), pairs)

    swap = [(0, 1), (1, 0)]
    both = jnp.stack([left_raw, right_raw])
    offset = line_offset.reshape(1, width)
    far = fetch(both, 3)
    mid = fetch(right_raw, 2)
    near = fetch(both, 1)
    beside = lax.ppermute(both, "det", swap)
    beside_offset = lax.ppermute(offset, "det", swap)
    far2, mid2, near2 = (lax.ppermute(v, "band", swap) for v in (far, mid, near))
    ins = [offset, beside_offset, left_raw, right_raw, beside, far, far2, near, near2, mid, mid2]
    specs = [VMEM, VMEM] + [ANY] * 9

    def copies(ins, strip, tile, det):
        band = lax.axis_index("band")

        def rows(flip):
            return pl.ds(pl.multiple_of(OMAX + (tile ^ flip) * lines, SUB), lines)

        def half(flip):
            return pl.ds(pl.multiple_of((det ^ flip) * width, LANES), width)

        _, _, left, right, beside, far, far2, near, near2, mid, mid2 = ins
        yield left, strip.at[0, rows(0), half(0)]
        yield right, strip.at[1, rows(0), half(0)]
        yield beside, strip.at[:, rows(0), half(1)]
        yield far, strip.at[:, rows(3), half(band)]
        yield far2, strip.at[:, rows(3), half(1 - band)]
        yield near, strip.at[:, rows(1), half(band)]
        yield near2, strip.at[:, rows(1), half(1 - band)]
        yield mid, strip.at[1, rows(2), half(band)]
        yield mid2, strip.at[1, rows(2), half(1 - band)]

    def offsets(ins, det):
        own, other = ins[0], ins[1]
        per = width // LANES
        result = []
        for chunk in range(dets * per):
            cols = slice((chunk % per) * LANES, (chunk % per + 1) * LANES)
            value = jnp.where(det == chunk // per, own[0:1, cols], other[0:1, cols])
            result.append(jnp.broadcast_to(value, (SUB, LANES)))
        return result

    plan = dict(
        lines=lines,
        blocks=tiles,
        two_sided=False,
        pad=0,
        copies=copies,
        n_copies=9,
        offsets=offsets,
        block_of=lambda partner, tile: partner,
    )
    return plan, ins, specs, dets * width


def shift_front(left_raw, right_raw, line_offset):
    count, dets = lax.axis_size("tile"), lax.axis_size("det")
    lines, width = left_raw.shape
    reach = REACH + 1
    own = lax.all_gather(jnp.stack([left_raw, right_raw]), "det")
    offset = lax.all_gather(line_offset, "det").reshape(1, dets * width)
    ins = [offset]
    for shift in range(-reach, reach + 1):
        if shift:
            pairs = [(i, i - shift) for i in range(count) if 0 <= i - shift < count]
            ins.append(lax.ppermute(own, "tile", pairs))
        else:
            ins.append(own)

    def copies(ins, strip, tile, det):
        for j in range(2 * reach + 1):
            for h in range(dets):
                rows = slice(OMAX + j * lines, OMAX + (j + 1) * lines)
                yield ins[1 + j].at[h], strip.at[:, rows, h * width : (h + 1) * width]

    def offsets(ins, det):
        return [
            jnp.broadcast_to(ins[0][0:1, c * LANES : (c + 1) * LANES], (SUB, LANES))
            for c in range(dets * width // LANES)
        ]

    plan = dict(
        lines=lines,
        blocks=2 * reach + 1,
        two_sided=True,
        pad=SUB,
        copies=copies,
        n_copies=(2 * reach + 1) * dets,
        offsets=offsets,
        block_of=lambda partner, tile: partner - tile + reach,
    )
    return plan, ins, [VMEM] + [ANY] * (2 * reach + 1), dets * width


def shards(left_raw, right_raw, line_offset, pair_count, pair_tile, pair_base):
    sizes = tuple(lax.axis_size(a) for a in ("tile", "det", "band"))
    front = xor_front if sizes == (4, 2, 2) else shift_front
    plan, ins, specs, cols = front(left_raw, right_raw, line_offset)
    return run_kernel(plan, ins, pair_count, pair_tile, pair_base, cols, specs)


def solution(mesh):
    return jax.shard_map(
        shards,
        mesh=mesh,
        in_specs=(
            P(("groups", "tile"), "det"),
            P(("groups", "tile"), "det"),
            P(("groups", "det")),
            P(("groups", "tile")),
            P(("groups", "tile"), None),
            P(("groups", "tile"), None),
        ),
        out_specs=P(("groups", "tile"), None, "det", None),
        check_vma=False,
    )
```

```python
import functools

import jax
import jax.numpy as jnp
from jax import lax
from jax.experimental import pallas as pl
from jax.experimental.pallas import tpu as pltpu
from jax.sharding import PartitionSpec as P

DISP = 128
WIN = 15
PMAX = 2
REACH = 2
OMAX = 8

REG = 0.1
SHARP = 30.0

LANES = 128
SUB = 8
BLKS = 4
STEPS = DISP // SUB
VIEWS = BLKS + STEPS - 1


def lane_gather(source, index):
    return jnp.take_along_axis(source, index, axis=1)


def row_gather(source, index):
    return jnp.take_along_axis(source, index, axis=0)


def stereo_kernel(plan, *refs):
    n_in = plan["n_in"]
    ins = refs[:n_in]
    count_ref, partner_ref, base_ref = refs[n_in : n_in + 3]
    out_ref = refs[n_in + 3]
    strip, tiles, left_rows, left_stats, raw_stats, right_rows, right_stats, sums, outs, sem = refs[
        n_in + 4 :
    ]
    lines = plan["lines"]
    two_sided = plan["two_sided"]
    pad = plan["pad"]
    blocks = plan["blocks"]
    det = lax.axis_index("det")
    tile = lax.axis_index("tile")
    n_win = WIN - 1 + SUB if two_sided else SUB + WIN // 2

    copies = []
    for source, target in plan["copies"](ins, strip, tile, det):
        copy = pltpu.make_async_copy(source, target, sem.at[len(copies)])
        copy.start()
        copies.append(copy)

    lane = lax.broadcasted_iota(jnp.int32, (SUB, LANES), 1)
    row = lax.broadcasted_iota(jnp.int32, (SUB, LANES), 0)
    zero = jnp.zeros((SUB, LANES), jnp.float32)
    chunks = out_ref.shape[-1] // LANES
    per = LANES // BLKS
    for plane in range(2):
        for chunk in range(chunks):
            cols = slice(chunk * LANES, (chunk + 1) * LANES)
            strip[plane, 0:OMAX, cols] = zero
            strip[plane, OMAX + blocks * lines : 2 * OMAX + blocks * lines, cols] = zero
    if pad:
        for plane in range(2):
            for blk in range(BLKS):
                tiles[plane, blk, 0:SUB, :] = zero
                tiles[plane, blk, SUB + lines : 2 * SUB + lines, :] = zero
    offsets = plan["offsets"](ins, det)
    for copy in copies:
        copy.wait()

    def resample(plane, block):
        for group in range(lines // SUB):
            start = block * lines + group * SUB
            natural = []
            for chunk in range(chunks):
                cols = slice(chunk * LANES, (chunk + 1) * LANES)
                want = row + offsets[chunk] + OMAX
                index = want & (SUB - 1)
                part = want >> 3
                picked = [
                    row_gather(
                        strip[plane, pl.ds(pl.multiple_of(start + SUB * k, SUB), SUB), cols], index
                    )
                    for k in range(3)
                ]
                natural.append(
                    jnp.where(part == 0, picked[0], jnp.where(part == 1, picked[1], picked[2]))
                )
            for blk in range(BLKS):
                index = (BLKS * lane + blk) & (LANES - 1)
                value = lane_gather(natural[0], index)
                for chunk in range(1, chunks):
                    value = jnp.where(
                        lane >= chunk * per, lane_gather(natural[chunk], index), value
                    )
                tiles[plane, blk, pad + group * SUB : pad + group * SUB + SUB, :] = value

    def row_at(win):
        if not two_sided:
            return win + det * (lines - 1 - 2 * win)
        if win < SUB + WIN // 2:
            return pad + SUB * det + win
        return pad + SUB * det - 1 - (win - SUB - WIN // 2)

    def load_row(plane, blk, win):
        return jnp.broadcast_to(tiles[plane, blk, pl.ds(row_at(win), 1), :], (SUB, LANES))

    def up(value, count):
        return jnp.where(lane >= count, pltpu.roll(value, count, 1), 0.0)

    def down(value, count):
        return jnp.where(lane < LANES - count, pltpu.roll(value, LANES - count, 1), 0.0)

    def down_wrapped(value, count):
        return jnp.where(lane >= LANES - count, pltpu.roll(value, LANES - count, 1), 0.0)

    def partials(values):
        first2 = values[0] + values[1]
        first3 = first2 + values[2]
        last2 = values[2] + values[3]
        return first2, first3, first3 + values[3], last2, values[1] + last2

    def across(values):
        first2, first3, full, last2, last3 = partials(values)
        mid = full + up(full, 1) + down(full, 1)
        return [
            mid + up(last3, 2),
            (mid + up(last2, 2)) + down(values[0], 2),
            (mid + up(values[3], 2)) + down(first2, 2),
            mid + down(first3, 2),
        ]

    def across_before(values):
        first2, first3, full, _, _ = partials(values)
        mid = down_wrapped(full, 1)
        return [
            mid,
            mid + down_wrapped(values[0], 2),
            mid + down_wrapped(first2, 2),
            mid + down_wrapped(first3, 2),
        ]

    def each_line(product):
        current = []
        for blk in range(BLKS):
            total = product(0, blk)
            for win in range(1, SUB):
                total = total + product(win, blk)
            current.append(total)
        before = None
        if two_sided:
            before = [[zero] * BLKS]
            for j in range(WIN // 2):
                before.append(
                    [
                        before[-1][blk] + product(SUB + WIN // 2 + j, blk)
                        for blk in range(BLKS)
                    ]
                )
        for line in range(SUB):
            if line:
                current = [current[blk] + product(SUB + line - 1, blk) for blk in range(BLKS)]
            if two_sided:
                yield line, [current[blk] + before[SUB - 1 - line][blk] for blk in range(BLKS)]
            else:
                yield line, current

    cell = 1.0 / (WIN * WIN)

    def stats(total, squares):
        mean = total * cell
        return mean, lax.rsqrt((squares * cell - mean * mean) + REG)

    resample(0, plan["block_of"](tile, tile))
    for win in range(n_win):
        for blk in range(BLKS):
            left_rows[win, blk] = load_row(0, blk, win)
    plain = each_line(lambda win, blk: left_rows[win, blk])
    square = each_line(lambda win, blk: left_rows[win, blk] * left_rows[win, blk])
    for (line, total), (_, squares) in zip(plain, square):
        total = across(total)
        squares = across(squares)
        for blk in range(BLKS):
            mean, gain = stats(total[blk], squares[blk])
            left_stats[0, line, blk] = mean
            left_stats[1, line, blk] = gain * SHARP
    for win in range(n_win):
        for blk in range(BLKS):
            left_rows[win, blk] = left_rows[win, blk] * cell

    for slot in range(PMAX):
        for chunk in range(chunks):
            out_ref[0, slot, :, chunk * LANES : (chunk + 1) * LANES] = zero

    def run_slot(slot, carry):
        base = base_ref[0, slot]
        resample(1, plan["block_of"](partner_ref[0, slot], tile))
        right = [[load_row(1, blk, win) for blk in range(BLKS)] for win in range(n_win)]
        plain = each_line(lambda win, blk: right[win][blk])
        square = each_line(lambda win, blk: right[win][blk] * right[win][blk])
        for (line, total), (_, squares) in zip(plain, square):
            for part, function in enumerate((across, across_before)):
                part_total = function(total)
                part_squares = function(squares)
                for blk in range(BLKS):
                    mean, gain = stats(part_total[blk], part_squares[blk])
                    raw_stats[part, 0, line, blk] = mean
                    raw_stats[part, 1, line, blk] = gain

        def make_view(view, carry):
            shift = view - (STEPS - 1) - base
            blk = shift & (BLKS - 1)
            moved = (blk - shift) >> 2
            turn = moved + (STEPS // BLKS) * row
            wraps = lane >= LANES - turn
            source = (lane - turn) & (LANES - 1)

            def turned(value):
                return lane_gather(value, source)

            for win in range(n_win):
                value = jnp.broadcast_to(
                    tiles[1, blk, pl.ds(row_at(win), 1), :], (SUB, LANES)
                )
                right_rows[view, win] = turned(jnp.where(wraps, 0.0, value))
            for kind in range(2):
                for line in range(SUB):
                    right_stats[view, kind, line] = turned(
                        jnp.where(
                            wraps, raw_stats[1, kind, line, blk], raw_stats[0, kind, line, blk]
                        )
                    )
            return carry

        lax.fori_loop(0, VIEWS, make_view, 0, unroll=True)
        for line in range(SUB):
            for blk in range(BLKS):
                sums[0, line, blk] = zero
                sums[1, line, blk] = zero

        def step_body(count, carry):
            view = count
            for line, value in each_line(
                lambda win, blk: left_rows[win, blk] * right_rows[view + blk, win]
            ):
                for blk, total in enumerate(across(value)):
                    cov = total - left_stats[0, line, blk] * right_stats[view + blk, 0, line]
                    weight = jnp.exp(
                        (cov * left_stats[1, line, blk]) * right_stats[view + blk, 1, line]
                    )
                    held = sums[0, line, blk]
                    sums[1, line, blk] = sums[1, line, blk] + held
                    sums[0, line, blk] = held + weight
            return carry

        lax.fori_loop(0, STEPS, step_body, 0, unroll=4)
        scale = (row * STEPS).astype(jnp.float32)
        for line in range(SUB):
            for blk in range(BLKS):
                weights = sums[0, line, blk]
                moments = sums[1, line, blk] + scale * weights
                weight_sum = jnp.sum(weights, axis=0, keepdims=True)
                moment_sum = jnp.sum(moments, axis=0, keepdims=True)
                value = (base.astype(jnp.float32) + moment_sum / weight_sum) / DISP
                target = line if two_sided else line + det * (SUB - 1 - 2 * line)
                outs[blk, pl.ds(target, 1), :] = value
        for chunk in range(chunks):
            index = chunk * per + (lane >> 2)
            value = lane_gather(outs[0], index)
            for blk in range(1, BLKS):
                value = jnp.where(
                    (lane & (BLKS - 1)) == blk, lane_gather(outs[blk], index), value
                )
            out_ref[0, slot, :, chunk * LANES : (chunk + 1) * LANES] = value
        return carry

    lax.fori_loop(0, jnp.minimum(count_ref[0], PMAX), run_slot, 0)


def run_kernel(plan, ins, pair_count, pair_tile, pair_base, cols, specs):
    lines = plan["lines"]
    blocks = plan["blocks"]
    n_win = WIN - 1 + SUB if plan["two_sided"] else SUB + WIN // 2
    plan = dict(plan, n_in=len(ins))
    smem = pl.BlockSpec(memory_space=pltpu.SMEM)
    f32 = jnp.float32
    return pl.pallas_call(
        functools.partial(stereo_kernel, plan),
        out_shape=jax.ShapeDtypeStruct((1, PMAX, SUB, cols), f32),
        in_specs=list(specs) + [smem, smem, smem],
        out_specs=pl.BlockSpec(memory_space=pltpu.VMEM),
        scratch_shapes=[
            pltpu.VMEM((2, blocks * lines + 2 * OMAX, cols), f32),
            pltpu.VMEM((2, BLKS, lines + 2 * plan["pad"], LANES), f32),
            pltpu.VMEM((n_win, BLKS, SUB, LANES), f32),
            pltpu.VMEM((2, SUB, BLKS, SUB, LANES), f32),
            pltpu.VMEM((2, 2, SUB, BLKS, SUB, LANES), f32),
            pltpu.VMEM((VIEWS, n_win, SUB, LANES), f32),
            pltpu.VMEM((VIEWS, 2, SUB, SUB, LANES), f32),
            pltpu.VMEM((2, SUB, BLKS, SUB, LANES), f32),
            pltpu.VMEM((BLKS, SUB, LANES), f32),
            pltpu.SemaphoreType.DMA((plan["n_copies"],)),
        ],
        compiler_params=pltpu.CompilerParams(vmem_limit_bytes=32 << 20),
        name="stereo",
    )(*ins, pair_count, pair_tile, pair_base)


ANY = pl.BlockSpec(memory_space=pl.ANY)
VMEM = pl.BlockSpec(memory_space=pltpu.VMEM)


def xor_front(left_raw, right_raw, line_offset):
    tiles, dets, bands = (lax.axis_size(a) for a in ("tile", "det", "band"))
    lines, width = left_raw.shape

    def fetch(value, flip):
        pairs = []
        for t in range(tiles):
            for d in range(dets):
                for b in range(bands):
                    source = (t * dets + d) * bands + b
                    target = ((t ^ flip) * dets + (d ^ b)) * bands + b
                    pairs.append((source, target))
        return lax.ppermute(value, ("tile", "det", "band"), pairs)

    swap = [(0, 1), (1, 0)]
    offset = jnp.broadcast_to(line_offset.astype(jnp.float32)[None], (SUB, width))
    slab = jnp.concatenate([left_raw, right_raw, offset])
    far, mid, near = (fetch(slab, flip) for flip in (3, 2, 1))
    beside = lax.ppermute(slab, "det", swap)
    far2, mid2, near2 = (lax.ppermute(v, "band", swap) for v in (far, mid, near))
    own = line_offset.reshape(1, width)
    ins = [own, beside, left_raw, right_raw, far, far2, near, near2, mid, mid2]
    specs = [VMEM, VMEM] + [ANY] * 8

    def copies(ins, strip, tile, det):
        band = lax.axis_index("band")

        def place(plane, flip, side):
            rows = pl.ds(pl.multiple_of(OMAX + (tile ^ flip) * lines, SUB), lines)
            half = pl.ds(pl.multiple_of((det ^ side) * width, LANES), width)
            return strip.at[plane, rows, half]

        def part(ref, plane):
            return ref.at[plane * lines : (plane + 1) * lines]

        _, beside, left, right, far, far2, near, near2, mid, mid2 = ins
        yield left, place(0, 0, 0)
        yield right, place(1, 0, 0)
        for plane in range(2):
            yield part(beside, plane), place(plane, 0, 1)
            for first, second, flip in ((far, far2, 3), (near, near2, 1), (mid, mid2, 2)):
                if plane or flip != 2:
                    yield part(first, plane), place(plane, flip, band)
                    yield part(second, plane), place(plane, flip, 1 - band)

    def offsets(ins, det):
        own, other = ins[0], ins[1]
        per = width // LANES
        result = []
        for chunk in range(dets * per):
            cols = slice((chunk % per) * LANES, (chunk % per + 1) * LANES)
            value = jnp.where(
                det == chunk // per,
                jnp.broadcast_to(own[0:1, cols], (SUB, LANES)),
                other[2 * lines : 2 * lines + SUB, cols].astype(jnp.int32),
            )
            result.append(value)
        return result

    plan = dict(
        lines=lines,
        blocks=tiles,
        two_sided=False,
        pad=0,
        copies=copies,
        n_copies=14,
        offsets=offsets,
        block_of=lambda partner, tile: partner,
    )
    return plan, ins, specs, dets * width


def shift_front(left_raw, right_raw, line_offset):
    count, dets = lax.axis_size("tile"), lax.axis_size("det")
    lines, width = left_raw.shape
    reach = REACH + 1
    own = lax.all_gather(jnp.stack([left_raw, right_raw]), "det")
    offset = lax.all_gather(line_offset, "det").reshape(1, dets * width)
    ins = [offset]
    for shift in range(-reach, reach + 1):
        if shift:
            pairs = [(i, i - shift) for i in range(count) if 0 <= i - shift < count]
            ins.append(lax.ppermute(own, "tile", pairs))
        else:
            ins.append(own)

    def copies(ins, strip, tile, det):
        for j in range(2 * reach + 1):
            for h in range(dets):
                rows = slice(OMAX + j * lines, OMAX + (j + 1) * lines)
                yield ins[1 + j].at[h], strip.at[:, rows, h * width : (h + 1) * width]

    def offsets(ins, det):
        return [
            jnp.broadcast_to(ins[0][0:1, c * LANES : (c + 1) * LANES], (SUB, LANES))
            for c in range(dets * width // LANES)
        ]

    plan = dict(
        lines=lines,
        blocks=2 * reach + 1,
        two_sided=True,
        pad=SUB,
        copies=copies,
        n_copies=(2 * reach + 1) * dets,
        offsets=offsets,
        block_of=lambda partner, tile: partner - tile + reach,
    )
    return plan, ins, [VMEM] + [ANY] * (2 * reach + 1), dets * width


def shards(left_raw, right_raw, line_offset, pair_count, pair_tile, pair_base):
    sizes = tuple(lax.axis_size(a) for a in ("tile", "det", "band"))
    front = xor_front if sizes == (4, 2, 2) else shift_front
    plan, ins, specs, cols = front(left_raw, right_raw, line_offset)
    return run_kernel(plan, ins, pair_count, pair_tile, pair_base, cols, specs)


def solution(mesh):
    return jax.shard_map(
        shards,
        mesh=mesh,
        in_specs=(
            P(("groups", "tile"), "det"),
            P(("groups", "tile"), "det"),
            P(("groups", "det")),
            P(("groups", "tile")),
            P(("groups", "tile"), None),
            P(("groups", "tile"), None),
        ),
        out_specs=P(("groups", "tile"), None, "det", None),
        check_vma=False,
    )
```

```python
import functools

import jax
import jax.numpy as jnp
from jax import lax
from jax.experimental import pallas as pl
from jax.experimental.pallas import tpu as pltpu
from jax.sharding import PartitionSpec as P

DISP = 128
WIN = 15
PMAX = 2
REACH = 2
OMAX = 8

REG = 0.1
SHARP = 30.0

LANES = 128
SUB = 8
BLKS = 4
STEPS = DISP // SUB
VIEWS = BLKS + STEPS - 1
GROUP = 4


def lane_gather(source, index):
    return jnp.take_along_axis(source, index, axis=1)


def row_gather(source, index):
    return jnp.take_along_axis(source, index, axis=0)


def stereo_kernel(plan, *refs):
    n_in = plan["n_in"]
    ins = refs[:n_in]
    table_any, out_ref = refs[n_in : n_in + 2]
    strip, tiles, left_rows, left_stats, raw_rows, raw_stats, right_rows, right_stats = refs[
        n_in + 2 : n_in + 10
    ]
    sums, outs, table_ref, sem = refs[n_in + 10 :]
    lines = plan["lines"]
    two_sided = plan["two_sided"]
    pad = plan["pad"]
    blocks = plan["blocks"]
    det = lax.axis_index("det")
    tile = lax.axis_index("tile")
    n_win = WIN - 1 + SUB if two_sided else SUB + WIN // 2

    copy = pltpu.make_async_copy(table_any, table_ref, sem)
    copy.start()

    lane = lax.broadcasted_iota(jnp.int32, (SUB, LANES), 1)
    row = lax.broadcasted_iota(jnp.int32, (SUB, LANES), 0)
    zero = jnp.zeros((SUB, LANES), jnp.float32)
    chunks = out_ref.shape[-1] // LANES
    per = LANES // BLKS
    for plane in range(2):
        for chunk in range(chunks):
            cols = slice(chunk * LANES, (chunk + 1) * LANES)
            strip[plane, 0:OMAX, cols] = zero
            strip[plane, OMAX + blocks * lines : 2 * OMAX + blocks * lines, cols] = zero
    if pad:
        for plane in range(2):
            for blk in range(BLKS):
                tiles[plane, blk, 0:SUB, :] = zero
                tiles[plane, blk, SUB + lines : 2 * SUB + lines, :] = zero
    offsets = plan["offsets"](ins, det)
    plan["fill"](ins, strip, tile, det)

    def resample(plane, block):
        for group in range(lines // SUB):
            start = block * lines + group * SUB
            natural = []
            for chunk in range(chunks):
                cols = slice(chunk * LANES, (chunk + 1) * LANES)
                want = row + offsets[chunk] + OMAX
                index = want & (SUB - 1)
                part = want >> 3
                picked = [
                    row_gather(
                        strip[plane, pl.ds(pl.multiple_of(start + SUB * k, SUB), SUB), cols], index
                    )
                    for k in range(3)
                ]
                natural.append(
                    jnp.where(part == 0, picked[0], jnp.where(part == 1, picked[1], picked[2]))
                )
            for blk in range(BLKS):
                index = (BLKS * lane + blk) & (LANES - 1)
                value = lane_gather(natural[0], index)
                for chunk in range(1, chunks):
                    value = jnp.where(
                        lane >= chunk * per, lane_gather(natural[chunk], index), value
                    )
                tiles[plane, blk, pad + group * SUB : pad + group * SUB + SUB, :] = value

    def row_at(win):
        if not two_sided:
            return win + det * (lines - 1 - 2 * win)
        if win < SUB + WIN // 2:
            return pad + SUB * det + win
        return pad + SUB * det - 1 - (win - SUB - WIN // 2)

    def load_row(plane, blk, win):
        return jnp.broadcast_to(tiles[plane, blk, pl.ds(row_at(win), 1), :], (SUB, LANES))

    def up(value, count):
        return jnp.where(lane >= count, pltpu.roll(value, count, 1), 0.0)

    def down(value, count):
        return jnp.where(lane < LANES - count, pltpu.roll(value, LANES - count, 1), 0.0)

    def down_wrapped(value, count):
        return jnp.where(lane >= LANES - count, pltpu.roll(value, LANES - count, 1), 0.0)

    def partials(values):
        first2 = values[0] + values[1]
        first3 = first2 + values[2]
        last2 = values[2] + values[3]
        return first2, first3, first3 + values[3], last2, values[1] + last2

    def across(values):
        first2, first3, full, last2, last3 = partials(values)
        mid = full + up(full, 1) + down(full, 1)
        return [
            mid + up(last3, 2),
            (mid + up(last2, 2)) + down(values[0], 2),
            (mid + up(values[3], 2)) + down(first2, 2),
            mid + down(first3, 2),
        ]

    def across_before(values):
        first2, first3, full, _, _ = partials(values)
        mid = down_wrapped(full, 1)
        return [
            mid,
            mid + down_wrapped(values[0], 2),
            mid + down_wrapped(first2, 2),
            mid + down_wrapped(first3, 2),
        ]

    def each_line(product):
        current = []
        for blk in range(BLKS):
            total = product(0, blk)
            for win in range(1, SUB):
                total = total + product(win, blk)
            current.append(total)
        before = None
        if two_sided:
            before = [[zero] * BLKS]
            for j in range(WIN // 2):
                before.append(
                    [
                        before[-1][blk] + product(SUB + WIN // 2 + j, blk)
                        for blk in range(BLKS)
                    ]
                )
        for line in range(SUB):
            if line:
                current = [current[blk] + product(SUB + line - 1, blk) for blk in range(BLKS)]
            if two_sided:
                yield line, [current[blk] + before[SUB - 1 - line][blk] for blk in range(BLKS)]
            else:
                yield line, current

    cell = 1.0 / (WIN * WIN)

    def stats(total, squares):
        mean = total * cell
        return mean, lax.rsqrt((squares * cell - mean * mean) + REG)

    resample(0, plan["block_of"](tile, tile))
    for win in range(n_win):
        for blk in range(BLKS):
            left_rows[win, blk] = load_row(0, blk, win)
    plain = each_line(lambda win, blk: left_rows[win, blk])
    square = each_line(lambda win, blk: left_rows[win, blk] * left_rows[win, blk])
    for (line, total), (_, squares) in zip(plain, square):
        total = across(total)
        squares = across(squares)
        for blk in range(BLKS):
            mean, gain = stats(total[blk], squares[blk])
            left_stats[0, line, blk] = mean
            left_stats[1, line, blk] = gain * SHARP
    for win in range(n_win):
        for blk in range(BLKS):
            left_rows[win, blk] = left_rows[win, blk] * cell

    copy.wait()
    for slot in range(PMAX):
        for chunk in range(chunks):
            out_ref[0, slot, :, chunk * LANES : (chunk + 1) * LANES] = zero

    def run_slot(slot, carry):
        base = table_ref[0, PMAX + slot]
        resample(1, plan["block_of"](table_ref[0, slot], tile))
        right = [[load_row(1, blk, win) for blk in range(BLKS)] for win in range(n_win)]
        for win in range(n_win):
            for blk in range(BLKS):
                raw_rows[win, blk] = right[win][blk]
        plain = each_line(lambda win, blk: right[win][blk])
        square = each_line(lambda win, blk: right[win][blk] * right[win][blk])
        for (line, total), (_, squares) in zip(plain, square):
            for part, function in enumerate((across, across_before)):
                part_total = function(total)
                part_squares = function(squares)
                for blk in range(BLKS):
                    mean, gain = stats(part_total[blk], part_squares[blk])
                    raw_stats[part, 0, line, blk] = mean
                    raw_stats[part, 1, line, blk] = gain

        def make_view(view, carry):
            shift = view - (STEPS - 1) - base
            blk = shift & (BLKS - 1)
            moved = (blk - shift) >> 2
            turn = moved + (STEPS // BLKS) * row
            wraps = lane >= LANES - turn
            source = (lane - turn) & (LANES - 1)

            def turned(value):
                return lane_gather(value, source)

            for win in range(n_win):
                right_rows[view, win] = turned(jnp.where(wraps, 0.0, raw_rows[win, blk]))
            for kind in range(2):
                for line in range(SUB):
                    right_stats[view, kind, line] = turned(
                        jnp.where(
                            wraps, raw_stats[1, kind, line, blk], raw_stats[0, kind, line, blk]
                        )
                    )
            return carry

        lax.fori_loop(0, VIEWS, make_view, 0, unroll=True)
        for line in range(SUB):
            for blk in range(BLKS):
                sums[0, line, blk] = zero
                sums[1, line, blk] = zero

        def step_body(group, carry):
            first = group * GROUP
            views = range(BLKS + GROUP - 1)

            def add(totals, win):
                left = [left_rows[win, blk] for blk in range(BLKS)]
                right = [right_rows[first + view, win] for view in views]
                terms = [
                    [left[blk] * right[step + blk] for blk in range(BLKS)] for step in range(GROUP)
                ]
                if totals is None:
                    return terms
                return [[t + v for t, v in zip(*pair)] for pair in zip(totals, terms)]

            current = None
            for win in range(SUB):
                current = add(current, win)
            before = [None]
            if two_sided:
                for j in range(WIN // 2):
                    before.append(add(before[-1], SUB + WIN // 2 + j))
            for line in range(SUB):
                if line:
                    current = add(current, SUB + line - 1)
                values = current
                if two_sided and line < SUB - 1:
                    values = [
                        [t + v for t, v in zip(*pair)]
                        for pair in zip(current, before[SUB - 1 - line])
                    ]
                mean_l = [left_stats[0, line, blk] for blk in range(BLKS)]
                gain_l = [left_stats[1, line, blk] for blk in range(BLKS)]
                mean_r = [right_stats[first + view, 0, line] for view in views]
                gain_r = [right_stats[first + view, 1, line] for view in views]
                weights = [sums[0, line, blk] for blk in range(BLKS)]
                moments = [sums[1, line, blk] for blk in range(BLKS)]
                for step in range(GROUP):
                    for blk, total in enumerate(across(values[step])):
                        cov = total - mean_l[blk] * mean_r[step + blk]
                        weight = jnp.exp((cov * gain_l[blk]) * gain_r[step + blk])
                        moments[blk] = moments[blk] + weights[blk]
                        weights[blk] = weights[blk] + weight
                for blk in range(BLKS):
                    sums[0, line, blk] = weights[blk]
                    sums[1, line, blk] = moments[blk]
            return carry

        lax.fori_loop(0, STEPS // GROUP, step_body, 0, unroll=True)
        scale = (row * STEPS).astype(jnp.float32)
        for line in range(SUB):
            for blk in range(BLKS):
                weights = sums[0, line, blk]
                moments = sums[1, line, blk] + scale * weights
                weight_sum = jnp.sum(weights, axis=0, keepdims=True)
                moment_sum = jnp.sum(moments, axis=0, keepdims=True)
                value = (base.astype(jnp.float32) + moment_sum / weight_sum) / DISP
                target = line if two_sided else line + det * (SUB - 1 - 2 * line)
                outs[blk, pl.ds(target, 1), :] = value
        for chunk in range(chunks):
            index = chunk * per + (lane >> 2)
            value = lane_gather(outs[0], index)
            for blk in range(1, BLKS):
                value = jnp.where(
                    (lane & (BLKS - 1)) == blk, lane_gather(outs[blk], index), value
                )
            out_ref[0, slot, :, chunk * LANES : (chunk + 1) * LANES] = value
        return carry

    lax.fori_loop(0, jnp.minimum(table_ref[0, 2 * PMAX], PMAX), run_slot, 0)


def run_kernel(plan, ins, pair_count, pair_tile, pair_base, cols):
    lines = plan["lines"]
    blocks = plan["blocks"]
    n_win = WIN - 1 + SUB if plan["two_sided"] else SUB + WIN // 2
    plan = dict(plan, n_in=len(ins))
    vmem = pl.BlockSpec(memory_space=pltpu.VMEM)
    anywhere = pl.BlockSpec(memory_space=pl.ANY)
    table = jnp.concatenate([pair_tile, pair_base, pair_count[None]], axis=1)
    f32 = jnp.float32
    return pl.pallas_call(
        functools.partial(stereo_kernel, plan),
        out_shape=jax.ShapeDtypeStruct((1, PMAX, SUB, cols), f32),
        in_specs=[vmem] * len(ins) + [anywhere],
        out_specs=vmem,
        scratch_shapes=[
            pltpu.VMEM((2, blocks * lines + 2 * OMAX, cols), f32),
            pltpu.VMEM((2, BLKS, lines + 2 * plan["pad"], LANES), f32),
            pltpu.VMEM((n_win, BLKS, SUB, LANES), f32),
            pltpu.VMEM((2, SUB, BLKS, SUB, LANES), f32),
            pltpu.VMEM((n_win, BLKS, SUB, LANES), f32),
            pltpu.VMEM((2, 2, SUB, BLKS, SUB, LANES), f32),
            pltpu.VMEM((VIEWS, n_win, SUB, LANES), f32),
            pltpu.VMEM((VIEWS, 2, SUB, SUB, LANES), f32),
            pltpu.VMEM((2, SUB, BLKS, SUB, LANES), f32),
            pltpu.VMEM((BLKS, SUB, LANES), f32),
            pltpu.SMEM(table.shape, jnp.int32),
            pltpu.SemaphoreType.DMA,
        ],
        compiler_params=pltpu.CompilerParams(vmem_limit_bytes=32 << 20),
        name="stereo",
    )(*ins, table)


def xor_front(left_raw, right_raw, line_offset):
    tiles, dets, bands = (lax.axis_size(a) for a in ("tile", "det", "band"))
    lines, width = left_raw.shape

    def fetch(value, flip):
        pairs = []
        for t in range(tiles):
            for d in range(dets):
                for b in range(bands):
                    source = (t * dets + d) * bands + b
                    target = ((t ^ flip) * dets + (d ^ b)) * bands + b
                    pairs.append((source, target))
        return lax.ppermute(value, ("tile", "det", "band"), pairs)

    swap = [(0, 1), (1, 0)]
    both = jnp.concatenate([left_raw, right_raw])
    far, mid, near = (fetch(both, flip) for flip in (3, 2, 1))
    held, line_offset = lax.optimization_barrier((both, line_offset))
    spread = jnp.broadcast_to(line_offset.astype(jnp.float32)[None], (SUB, width))
    slab = jnp.concatenate([held, spread])
    beside = lax.ppermute(slab, "det", swap)
    far2, mid2, near2 = (lax.ppermute(v, "band", swap) for v in (far, mid, near))
    ins = [slab, beside, mid, mid2, near, near2, far, far2]

    def fill(ins, strip, tile, det):
        band = lax.axis_index("band")

        def place(ref, plane, flip, side):
            rows = pl.ds(pl.multiple_of(OMAX + (tile ^ flip) * lines, SUB), lines)
            half = pl.ds(pl.multiple_of((det ^ side) * width, LANES), width)
            strip[plane, rows, half] = ref[plane * lines : (plane + 1) * lines, :]

        slab, beside, mid, mid2, near, near2, far, far2 = ins
        for plane in range(2):
            place(slab, plane, 0, 0)
            place(beside, plane, 0, 1)
            for first, second, flip in ((far, far2, 3), (near, near2, 1), (mid, mid2, 2)):
                if plane or flip != 2:
                    place(first, plane, flip, band)
                    place(second, plane, flip, 1 - band)

    def offsets(ins, det):
        own, other = ins[0], ins[1]
        per = width // LANES
        result = []
        for chunk in range(dets * per):
            cols = slice((chunk % per) * LANES, (chunk % per + 1) * LANES)
            rows = slice(2 * lines, 2 * lines + SUB)
            value = jnp.where(det == chunk // per, own[rows, cols], other[rows, cols])
            result.append(value.astype(jnp.int32))
        return result

    plan = dict(
        lines=lines,
        blocks=tiles,
        two_sided=False,
        pad=0,
        fill=fill,
        offsets=offsets,
        block_of=lambda partner, tile: partner,
    )
    return plan, ins, dets * width


def shift_front(left_raw, right_raw, line_offset):
    count, dets = lax.axis_size("tile"), lax.axis_size("det")
    lines, width = left_raw.shape
    reach = REACH + 1
    own = lax.all_gather(jnp.stack([left_raw, right_raw]), "det")
    offset = lax.all_gather(line_offset, "det").reshape(1, dets * width)
    ins = [offset]
    for shift in range(-reach, reach + 1):
        if shift:
            pairs = [(i, i - shift) for i in range(count) if 0 <= i - shift < count]
            ins.append(lax.ppermute(own, "tile", pairs))
        else:
            ins.append(own)

    def fill(ins, strip, tile, det):
        for j in range(2 * reach + 1):
            rows = slice(OMAX + j * lines, OMAX + (j + 1) * lines)
            for h in range(dets):
                for plane in range(2):
                    strip[plane, rows, h * width : (h + 1) * width] = ins[1 + j][h, plane]

    def offsets(ins, det):
        return [
            jnp.broadcast_to(ins[0][0:1, c * LANES : (c + 1) * LANES], (SUB, LANES))
            for c in range(dets * width // LANES)
        ]

    plan = dict(
        lines=lines,
        blocks=2 * reach + 1,
        two_sided=True,
        pad=SUB,
        fill=fill,
        offsets=offsets,
        block_of=lambda partner, tile: partner - tile + reach,
    )
    return plan, ins, dets * width


def shards(left_raw, right_raw, line_offset, pair_count, pair_tile, pair_base):
    sizes = tuple(lax.axis_size(a) for a in ("tile", "det", "band"))
    front = xor_front if sizes == (4, 2, 2) else shift_front
    plan, ins, cols = front(left_raw, right_raw, line_offset)
    return run_kernel(plan, ins, pair_count, pair_tile, pair_base, cols)


def solution(mesh):
    return jax.shard_map(
        shards,
        mesh=mesh,
        in_specs=(
            P(("groups", "tile"), "det"),
            P(("groups", "tile"), "det"),
            P(("groups", "det")),
            P(("groups", "tile")),
            P(("groups", "tile"), None),
            P(("groups", "tile"), None),
        ),
        out_specs=P(("groups", "tile"), None, "det", None),
        check_vma=False,
    )
```

```python
import functools

import jax
import jax.numpy as jnp
from jax import lax
from jax.experimental import pallas as pl
from jax.experimental.pallas import tpu as pltpu
from jax.sharding import PartitionSpec as P

DISP = 128
WIN = 15
PMAX = 2
REACH = 2
OMAX = 8

REG = 0.1
SHARP = 30.0

LANES = 128
SUB = 8
BLKS = 8
SPOTS = LANES // 2
STEPS = 8
SIDE = WIN // 2
VIEWS = BLKS + STEPS - 1
TOGETHER = 4


def lane_gather(source, index):
    return jnp.take_along_axis(source, index, axis=1)


def row_gather(source, index):
    return jnp.take_along_axis(source, index, axis=0)


def stereo_kernel(plan, *refs):
    n_in = plan["n_in"]
    ins = refs[:n_in]
    table_any, out_ref = refs[n_in : n_in + 2]
    strip, tiles, left_rows, left_stats, raw_rows, raw_stats = refs[n_in + 2 : n_in + 8]
    right_rows, right_stats, outs, table_ref, sem = refs[n_in + 8 :]
    lines = plan["lines"]
    two_sided = plan["two_sided"]
    pad = plan["pad"]
    blocks = plan["blocks"]
    det = lax.axis_index("det")
    tile = lax.axis_index("tile")
    n_win = SUB + 2 * SIDE if two_sided else SUB + SIDE

    copy = pltpu.make_async_copy(table_any, table_ref, sem)
    copy.start()

    lane = lax.broadcasted_iota(jnp.int32, (SUB, LANES), 1)
    row = lax.broadcasted_iota(jnp.int32, (SUB, LANES), 0)
    zero = jnp.zeros((SUB, LANES), jnp.float32)
    chunks = out_ref.shape[-1] // LANES
    per = LANES // BLKS
    spot = lane & (SPOTS - 1)
    half = lane >> 6
    for plane in range(2):
        for chunk in range(chunks):
            cols = slice(chunk * LANES, (chunk + 1) * LANES)
            strip[plane, 0:OMAX, cols] = zero
            strip[plane, OMAX + blocks * lines : 2 * OMAX + blocks * lines, cols] = zero
    if pad:
        for plane in range(2):
            for blk in range(BLKS):
                tiles[plane, blk, 0:SUB, :] = zero
                tiles[plane, blk, SUB + lines : 2 * SUB + lines, :] = zero
    offsets = plan["offsets"](ins, det)
    plan["fill"](ins, strip, tile, det)

    def resample(plane, block):
        for group in range(lines // SUB):
            start = block * lines + group * SUB
            natural = []
            for chunk in range(chunks):
                cols = slice(chunk * LANES, (chunk + 1) * LANES)
                want = row + offsets[chunk] + OMAX
                index = want & (SUB - 1)
                part = want >> 3
                picked = [
                    row_gather(
                        strip[plane, pl.ds(pl.multiple_of(start + SUB * k, SUB), SUB), cols], index
                    )
                    for k in range(3)
                ]
                natural.append(
                    jnp.where(part == 0, picked[0], jnp.where(part == 1, picked[1], picked[2]))
                )
            for blk in range(BLKS):
                index = (BLKS * spot + blk) & (LANES - 1)
                value = lane_gather(natural[0], index)
                for chunk in range(1, chunks):
                    value = jnp.where(
                        spot >= chunk * per, lane_gather(natural[chunk], index), value
                    )
                tiles[plane, blk, pad + group * SUB : pad + group * SUB + SUB, :] = value

    def row_at(win):
        if not two_sided:
            return win + det * (lines - 1 - 2 * win)
        if win < SUB + SIDE:
            return pad + SUB * det + win
        return pad + SUB * det - 1 - (win - SUB - SIDE)

    def load_row(ref, blk, win):
        return jnp.broadcast_to(ref[blk, pl.ds(row_at(win), 1), :], (SUB, LANES))

    def before(value):
        return pltpu.roll(value, 1, 1)

    def after(value):
        return pltpu.roll(value, LANES - 1, 1)

    def window_parts(wide):
        core = wide[SIDE]
        for blk in range(1, BLKS):
            core = core + wide[SIDE + blk]
        low, high = [None] * BLKS, [None] * BLKS
        for k in range(SIDE):
            value = wide[SIDE - 1 - k]
            low[BLKS - 2 - k] = value if k == 0 else low[BLKS - 1 - k] + value
            value = wide[SIDE + BLKS + k]
            high[k + 1] = value if k == 0 else high[k] + value
        return core, low, high

    def plus(first, second):
        return first if second is None else first + second

    def across(inner):
        first, last = [inner[0]], [inner[-1]]
        for k in range(1, BLKS):
            first.append(first[-1] + inner[k])
            if k < SIDE:
                last.append(last[-1] + inner[BLKS - 1 - k])
        result = [first[-1]] * BLKS
        for k in range(SIDE):
            low = jnp.where(spot >= 1, before(last[k]), 0.0)
            high = jnp.where(spot < SPOTS - 1, after(first[k]), 0.0)
            result[BLKS - 2 - k] = result[BLKS - 2 - k] + low
            result[k + 1] = result[k + 1] + high
        return result

    cell = 1.0 / (WIN * WIN)

    def tile_stats(rows, gain_scale):
        totals = []
        for square in (False, True):
            columns = []
            for blk in range(BLKS):
                total = None
                for win in range(n_win):
                    value = rows[win][blk]
                    if square:
                        value = value * value
                    if win >= SUB + SIDE:
                        value = jnp.where(row < SUB - 1 - (win - SUB - SIDE), value, 0.0)
                    elif win >= SUB:
                        value = jnp.where(row > win - SUB, value, 0.0)
                    total = plus(value, total)
                columns.append(total)
            wide = [
                jnp.where(spot >= 1, before(columns[blk]), 0.0) for blk in range(1, BLKS)
            ] + columns + [after(columns[blk]) for blk in range(BLKS - 1)]
            core, low, high = window_parts(wide)
            main, ahead = [], []
            for blk in range(BLKS):
                value = plus(core, low[blk])
                if high[blk] is None:
                    ahead.append(zero)
                else:
                    value = value + jnp.where(spot < SPOTS - 1, high[blk], 0.0)
                    ahead.append(jnp.where(spot == SPOTS - 1, high[blk], 0.0))
                main.append(value)
            totals.append((main, ahead))
        result = []
        for part in range(2):
            means, gains = [], []
            for blk in range(BLKS):
                mean = totals[0][part][blk] * cell
                variance = totals[1][part][blk] * cell - mean * mean
                means.append(mean)
                gains.append(lax.rsqrt(variance + REG) * gain_scale)
            result.append((means, gains))
        return result

    resample(0, plan["block_of"](tile, tile))
    left = [[load_row(tiles.at[0], blk, win) for blk in range(BLKS)] for win in range(n_win)]
    for kind, values in enumerate(tile_stats(left, SHARP)[0]):
        for blk in range(BLKS):
            for line in range(SUB):
                left_stats[kind, line, blk] = jnp.broadcast_to(
                    values[blk][line : line + 1, :], (SUB, LANES)
                )
    for win in range(n_win):
        for blk in range(BLKS):
            left_rows[win, blk] = left[win][blk] * cell

    copy.wait()
    for slot in range(PMAX):
        for chunk in range(chunks):
            out_ref[0, slot, :, chunk * LANES : (chunk + 1) * LANES] = zero

    def run_slot(slot, carry):
        base = table_ref[0, PMAX + slot]
        resample(1, plan["block_of"](table_ref[0, slot], tile))
        right = [[load_row(tiles.at[1], blk, win) for blk in range(BLKS)] for win in range(n_win)]
        for win in range(n_win):
            for blk in range(BLKS):
                raw_rows[win, blk] = right[win][blk]
        for part, pair in enumerate(tile_stats(right, 1.0)):
            for kind, values in enumerate(pair):
                for blk in range(BLKS):
                    raw_stats[part, kind, blk] = values[blk]

        for view in range(VIEWS):
            shift = view - (STEPS - 1) - base
            blk = shift & (BLKS - 1)
            turn = ((blk - shift) >> 3) + half + 2 * row
            wraps = spot >= SPOTS - turn
            source = ((lane - turn) & (SPOTS - 1)) + SPOTS * half
            for win in range(n_win):
                value = jnp.where(wraps, 0.0, raw_rows[win, blk])
                right_rows[view, win] = lane_gather(value, source)
            for kind in range(2):
                for line in range(SUB):
                    main, ahead = (
                        jnp.broadcast_to(
                            raw_stats[part, kind, blk, pl.ds(line, 1), :], (SUB, LANES)
                        )
                        for part in range(2)
                    )
                    right_stats[view, kind, line] = lane_gather(
                        jnp.where(wraps, ahead, main), source
                    )

        def add(totals, win, first, count):
            left = [left_rows[win, blk] for blk in range(BLKS)]
            right = [right_rows[first + view, win] for view in range(BLKS + count - 1)]
            terms = [[left[blk] * right[step + blk] for blk in range(BLKS)] for step in range(count)]
            return terms if totals is None else sums_of(totals, terms)

        def sums_of(totals, terms):
            return [[t + v for t, v in zip(*pair)] for pair in zip(totals, terms)]

        current = []
        for first in range(0, STEPS, TOGETHER):
            totals = None
            for win in range(SUB):
                totals = add(totals, win, first, TOGETHER)
            current += totals
        lower = [None]
        if two_sided:
            for j in range(SIDE):
                lower.append(add(lower[-1], SUB + SIDE + j, 0, STEPS))
        scale = (2 * BLKS * row + BLKS * half).astype(jnp.float32)
        for line in range(SUB):
            left = [left_rows[SUB + line - 1, blk] for blk in range(BLKS)]
            right = [right_rows[view, SUB + line - 1] for view in range(VIEWS)]
            mean_l = [left_stats[0, line, blk] for blk in range(BLKS)]
            gain_l = [left_stats[1, line, blk] for blk in range(BLKS)]
            weights, moments = [None] * BLKS, [None] * BLKS
            for step in range(STEPS):
                if line:
                    current[step] = [
                        current[step][blk] + left[blk] * right[step + blk] for blk in range(BLKS)
                    ]
                values = current[step]
                if two_sided and line < SUB - 1:
                    values = sums_of([values], [lower[SUB - 1 - line][step]])[0]
                mean_r = [right_stats[step + blk, 0, line] for blk in range(BLKS)]
                gain_r = [right_stats[step + blk, 1, line] for blk in range(BLKS)]
                for blk, total in enumerate(across(values)):
                    cov = total - mean_l[blk] * mean_r[blk]
                    weight = jnp.exp((cov * gain_l[blk]) * gain_r[blk])
                    if step == 0:
                        weights[blk] = weight
                    else:
                        moments[blk] = plus(weights[blk], moments[blk])
                        weights[blk] = weights[blk] + weight
            target = pl.ds(line if two_sided else line + det * (SUB - 1 - 2 * line), 1)
            for blk in range(BLKS):
                moment = moments[blk] + scale * weights[blk]
                outs[0, blk, target, :] = jnp.sum(weights[blk], axis=0, keepdims=True)
                outs[1, blk, target, :] = jnp.sum(moment, axis=0, keepdims=True)
        values = []
        for blk in range(BLKS):
            weights, moments = (v + pltpu.roll(v, SPOTS, 1) for v in (outs[0, blk], outs[1, blk]))
            values.append((base.astype(jnp.float32) + moments / weights) / DISP)
        for chunk in range(chunks):
            index = chunk * per + (lane >> 3)
            value = lane_gather(values[0], index)
            for blk in range(1, BLKS):
                value = jnp.where(
                    (lane & (BLKS - 1)) == blk, lane_gather(values[blk], index), value
                )
            out_ref[0, slot, :, chunk * LANES : (chunk + 1) * LANES] = value
        return carry

    lax.fori_loop(0, jnp.minimum(table_ref[0, 2 * PMAX], PMAX), run_slot, 0)


def run_kernel(plan, ins, pair_count, pair_tile, pair_base, cols):
    lines = plan["lines"]
    blocks = plan["blocks"]
    n_win = SUB + 2 * SIDE if plan["two_sided"] else SUB + SIDE
    plan = dict(plan, n_in=len(ins))
    vmem = pl.BlockSpec(memory_space=pltpu.VMEM)
    anywhere = pl.BlockSpec(memory_space=pl.ANY)
    table = jnp.concatenate([pair_tile, pair_base, pair_count[None]], axis=1)
    f32 = jnp.float32
    return pl.pallas_call(
        functools.partial(stereo_kernel, plan),
        out_shape=jax.ShapeDtypeStruct((1, PMAX, SUB, cols), f32),
        in_specs=[vmem] * len(ins) + [anywhere],
        out_specs=vmem,
        scratch_shapes=[
            pltpu.VMEM((2, blocks * lines + 2 * OMAX, cols), f32),
            pltpu.VMEM((2, BLKS, lines + 2 * plan["pad"], LANES), f32),
            pltpu.VMEM((n_win, BLKS, SUB, LANES), f32),
            pltpu.VMEM((2, SUB, BLKS, SUB, LANES), f32),
            pltpu.VMEM((n_win, BLKS, SUB, LANES), f32),
            pltpu.VMEM((2, 2, BLKS, SUB, LANES), f32),
            pltpu.VMEM((VIEWS, n_win, SUB, LANES), f32),
            pltpu.VMEM((VIEWS, 2, SUB, SUB, LANES), f32),
            pltpu.VMEM((2, BLKS, SUB, LANES), f32),
            pltpu.SMEM(table.shape, jnp.int32),
            pltpu.SemaphoreType.DMA,
        ],
        compiler_params=pltpu.CompilerParams(vmem_limit_bytes=32 << 20),
        name="stereo",
    )(*ins, table)


def xor_front(left_raw, right_raw, line_offset):
    tiles, dets, bands = (lax.axis_size(a) for a in ("tile", "det", "band"))
    lines, width = left_raw.shape

    def fetch(value, flip):
        pairs = []
        for t in range(tiles):
            for d in range(dets):
                for b in range(bands):
                    source = (t * dets + d) * bands + b
                    target = ((t ^ flip) * dets + (d ^ b)) * bands + b
                    pairs.append((source, target))
        return lax.ppermute(value, ("tile", "det", "band"), pairs)

    swap = [(0, 1), (1, 0)]
    both = jnp.concatenate([left_raw, right_raw])
    far, mid, near = (fetch(both, flip) for flip in (3, 2, 1))
    held, line_offset = lax.optimization_barrier((both, line_offset))
    spread = jnp.broadcast_to(line_offset.astype(jnp.float32)[None], (SUB, width))
    slab = jnp.concatenate([held, spread])
    beside = lax.ppermute(slab, "det", swap)
    far2, mid2, near2 = (lax.ppermute(v, "band", swap) for v in (far, mid, near))
    ins = [slab, beside, mid, mid2, near, near2, far, far2]

    def fill(ins, strip, tile, det):
        band = lax.axis_index("band")

        def place(ref, plane, flip, side):
            rows = pl.ds(pl.multiple_of(OMAX + (tile ^ flip) * lines, SUB), lines)
            half = pl.ds(pl.multiple_of((det ^ side) * width, LANES), width)
            strip[plane, rows, half] = ref[plane * lines : (plane + 1) * lines, :]

        slab, beside, mid, mid2, near, near2, far, far2 = ins
        for plane in range(2):
            place(slab, plane, 0, 0)
            place(beside, plane, 0, 1)
            for first, second, flip in ((far, far2, 3), (near, near2, 1), (mid, mid2, 2)):
                if plane or flip != 2:
                    place(first, plane, flip, band)
                    place(second, plane, flip, 1 - band)

    def offsets(ins, det):
        own, other = ins[0], ins[1]
        per = width // LANES
        result = []
        for chunk in range(dets * per):
            cols = slice((chunk % per) * LANES, (chunk % per + 1) * LANES)
            rows = slice(2 * lines, 2 * lines + SUB)
            value = jnp.where(det == chunk // per, own[rows, cols], other[rows, cols])
            result.append(value.astype(jnp.int32))
        return result

    plan = dict(
        lines=lines,
        blocks=tiles,
        two_sided=False,
        pad=0,
        fill=fill,
        offsets=offsets,
        block_of=lambda partner, tile: partner,
    )
    return plan, ins, dets * width


def shift_front(left_raw, right_raw, line_offset):
    count, dets = lax.axis_size("tile"), lax.axis_size("det")
    lines, width = left_raw.shape
    reach = REACH + 1
    own = lax.all_gather(jnp.stack([left_raw, right_raw]), "det")
    offset = lax.all_gather(line_offset, "det").reshape(1, dets * width)
    ins = [offset]
    for shift in range(-reach, reach + 1):
        if shift:
            pairs = [(i, i - shift) for i in range(count) if 0 <= i - shift < count]
            ins.append(lax.ppermute(own, "tile", pairs))
        else:
            ins.append(own)

    def fill(ins, strip, tile, det):
        for j in range(2 * reach + 1):
            rows = slice(OMAX + j * lines, OMAX + (j + 1) * lines)
            for h in range(dets):
                for plane in range(2):
                    strip[plane, rows, h * width : (h + 1) * width] = ins[1 + j][h, plane]

    def offsets(ins, det):
        return [
            jnp.broadcast_to(ins[0][0:1, c * LANES : (c + 1) * LANES], (SUB, LANES))
            for c in range(dets * width // LANES)
        ]

    plan = dict(
        lines=lines,
        blocks=2 * reach + 1,
        two_sided=True,
        pad=SUB,
        fill=fill,
        offsets=offsets,
        block_of=lambda partner, tile: partner - tile + reach,
    )
    return plan, ins, dets * width


def shards(left_raw, right_raw, line_offset, pair_count, pair_tile, pair_base):
    sizes = tuple(lax.axis_size(a) for a in ("tile", "det", "band"))
    front = xor_front if sizes == (4, 2, 2) else shift_front
    plan, ins, cols = front(left_raw, right_raw, line_offset)
    return run_kernel(plan, ins, pair_count, pair_tile, pair_base, cols)


def solution(mesh):
    return jax.shard_map(
        shards,
        mesh=mesh,
        in_specs=(
            P(("groups", "tile"), "det"),
            P(("groups", "tile"), "det"),
            P(("groups", "det")),
            P(("groups", "tile")),
            P(("groups", "tile"), None),
            P(("groups", "tile"), None),
        ),
        out_specs=P(("groups", "tile"), None, "det", None),
        check_vma=False,
    )
```
